256 devices in a mesh: layer: 8 (over z), latent: 32 (over x, y, core).
Axes of the slice: x: 4, y: 4, z: 8, core: 2. Of those that a mesh axis runs over, the one named last changes fastest.
Arguments:
- resid: bfloat16 [8, 1024, 4096], P('layer', 'latent'), may hold values from -6 to 6
- mlp_out: bfloat16 [8, 1024, 4096], P('layer', 'latent'), may hold values from -6 to 6
- enc_w: bfloat16 [8, 4096, 4096], P('layer', None, 'latent'), may hold values from -0.09375 to 0.09375
- enc_b: float32 [8, 4096], P('layer', 'latent'), may hold values from -3 to 3
- dec_w: bfloat16 [8, 8, 4096, 4096], P('layer', None, 'latent'), may hold values from -0.03125 to 0.03125
Outputs:
- error: bfloat16 [8, 1024, 4096], P('layer', 'latent')
The draws below stay inside these ranges and needn't reach their ends.
All inputs are finite; a program needn't handle non-finite values.
Results may differ from the reference program's by a relative error of at most 0.0034.
Values may be sent and summed in bfloat16 or wider, within the bound.
A program may use at most 128 MiB of HBM per device.

```python
import jax
import jax.numpy as jnp

D = 4096
F = 4096
LAYERS = 8
TOKENS = 1024


def shard_levels(stream_key, dims, shards, low, largest):
    factor_of = 1.0
    for dim, blocks in shards:
        draws = jax.random.uniform(jax.random.fold_in(jax.random.fold_in(stream_key, 6), dim), (blocks,), jnp.float32, low / len(shards), largest / len(shards))
        factor_of = factor_of * jnp.repeat(jnp.exp(draws), dims[dim] // blocks).reshape((-1,) + (1,) * (len(dims) - 1 - dim))
    return factor_of


def noise(rng, dims, deviation, reach, cuts=(), held_as=jnp.bfloat16):
    factor_of = shard_levels(rng, dims, cuts, -0.22, 0.18) if cuts else 1.0
    drawn = jax.random.normal(rng, dims, jnp.float32) * deviation * factor_of
    return jnp.minimum(jnp.maximum(drawn, -reach), reach).astype(held_as)


def setup_inputs(seed: int = 0) -> dict:
    splits = jax.random.split(jax.random.key(seed), 6)
    resid = noise(splits[0], (LAYERS, TOKENS, D), 1.0, 6.0, ((0, 8), (1, 32)))
    mlp_out = noise(splits[1], (LAYERS, TOKENS, D), 1.0, 6.0, ((0, 8), (1, 32)))
    enc_w = noise(splits[2], (LAYERS, D, F), D ** -0.5, 0.09375, ((0, 8), (2, 32)))
    enc_b = noise(splits[3], (LAYERS, F), 0.5, 3.0, ((0, 8), (1, 32)), jnp.float32)
    dec_w = noise(splits[4], (LAYERS, LAYERS, F, D), (LAYERS * F) ** -0.5, 0.03125, ((0, 8), (2, 32)))
    return {"resid": resid, "mlp_out": mlp_out, "enc_w": enc_w, "enc_b": enc_b, "dec_w": dec_w}


def reference(resid, mlp_out, enc_w, enc_b, dec_w):
    latents = []
    for source in range(LAYERS):
        pre = jnp.dot(resid[source], enc_w[source], preferred_element_type=jnp.float32) + enc_b[source]
        latents.append(jnp.maximum(pre, 0.0).astype(jnp.bfloat16))
    errors = []
    for target in range(LAYERS):
        recon = jnp.zeros((TOKENS, D), jnp.float32)
        for source in range(target + 1):
            recon = recon + jnp.dot(latents[source], dec_w[target, source], preferred_element_type=jnp.float32)
        errors.append((mlp_out[target].astype(jnp.float32) - recon).astype(jnp.bfloat16))
    return jnp.stack(errors)
```

```python
import functools

import jax
import jax.numpy as jnp
from jax import lax
from jax.experimental import pallas as pl
from jax.experimental.pallas import tpu as pltpu
from jax.sharding import PartitionSpec as P

MESH = pl.DeviceIdType.MESH
LAYERS = 8
SIDE = 4
CHUNKS = 2
ROWS = 16
D = 4096
HALF = 2048
QUARTER = 1024
LANES = 128
TILE = 512
OFFSETS = (1, SIDE - 1, 2)
FORWARD = 4
BACKWARD = 3


def kernel(
    resid, mlp, enc, bias, dec, out,
    R, WE, BE, WD, L, ACC, S, TA, TB, VA, VB, UA, UB, MV, OV,
    ag1_s, ag1_r, ag2_s, ag2_r, w_s, w_r, d_s, d_r, zf_s, zf_r, zb_s, zb_r,
    rs1_s, rs1_r, rs2_s, rs2_r, own_sem, loc_sem, dloc_sem, out_sem,
):
    z = lax.axis_index("layer")
    index = lax.axis_index("latent")
    core = lax.rem(index, 2)
    y = lax.rem(lax.div(index, 2), SIDE)
    x = lax.div(index, 2 * SIDE)

    def at_chip(px, py):
        return {"layer": z, "latent": (px * SIDE + py) * 2 + core}

    def at_layer(pz):
        return {"layer": pz, "latent": index}

    partner = {"layer": z, "latent": index + 1 - 2 * core}

    def move(v, o):
        return lax.rem(v + o, SIDE)

    def remote(src, dst, ss, rs, where):
        return pltpu.make_async_remote_copy(
            src_ref=src, dst_ref=dst, send_sem=ss, recv_sem=rs,
            device_id=where, device_id_type=MESH,
        )

    up, down = lax.rem(z + 1, LAYERS), lax.rem(z + LAYERS - 1, LAYERS)

    barrier = pltpu.get_barrier_semaphore()
    friends = [partner, at_layer(up), at_layer(down)]
    friends += [at_chip(move(x, o), y) for o in OFFSETS]
    friends += [at_chip(x, move(y, o)) for o in OFFSETS]
    for friend in friends:
        pl.semaphore_signal(barrier, inc=1, device_id=friend, device_id_type=MESH)
    pl.semaphore_wait(barrier, len(friends))

    def ag1(q, h, j):
        cols = pl.ds(h * HALF, HALF)
        o = OFFSETS[j]
        where = at_chip(move(x, o), y) if h == 0 else at_chip(x, move(y, o))
        return remote(
            resid.at[0, pl.ds(q * ROWS, ROWS), cols], R.at[q, x, y, :, cols],
            ag1_s.at[q, h, j], ag1_r.at[q, h, j], where,
        )

    def ag1_start(q):
        for j in range(3):
            for h in range(2):
                ag1(q, h, j).start()

    def ag1_wait(q, h):
        cols = pl.ds(h * HALF, HALF)
        for j in range(3):
            back = SIDE - OFFSETS[j]
            slot = R.at[q, move(x, back), y, :, cols] if h == 0 else R.at[q, x, move(y, back), :, cols]
            remote(slot, slot, ag1_s.at[q, h, j], ag1_r.at[q, h, j], partner).wait_recv()

    def lines(q, h, back, cols):
        if h == 0:
            return R.at[q, :, move(y, back), :, cols]
        return R.at[q, move(x, back), :, :, cols]

    def ag2(q, h, direction, piece):
        step = 1 if direction == 0 else SIDE - 1
        first = direction if piece != 1 else 1 - direction
        cols = pl.ds(h * HALF + first * QUARTER, QUARTER)
        back = 0 if piece < 2 else SIDE - step
        where = at_chip(x, move(y, step)) if h == 0 else at_chip(move(x, step), y)
        block = lines(q, h, back, cols)
        return remote(block, block, ag2_s.at[q, h, direction, piece], ag2_r.at[q, h, direction, piece], where)

    def ag2_arrive(q, h, direction, piece):
        step = 1 if direction == 0 else SIDE - 1
        first = direction if piece != 1 else 1 - direction
        cols = pl.ds(h * HALF + first * QUARTER, QUARTER)
        back = SIDE - step if piece < 2 else 2
        block = lines(q, h, back, cols)
        remote(block, block, ag2_s.at[q, h, direction, piece], ag2_r.at[q, h, direction, piece], partner).wait_recv()

    def ag2_start(q, h):
        for piece in range(2):
            for direction in range(2):
                ag2(q, h, direction, piece).start()

    def ag2_relay(q):
        for h in range(2):
            for direction in range(2):
                ag2_arrive(q, h, direction, 0)
                ag2(q, h, direction, 2).start()

    def ag2_rest(q):
        for piece in (1, 2):
            for h in range(2):
                for direction in range(2):
                    ag2_arrive(q, h, direction, piece)

    mine = pl.ds(pl.multiple_of(core * LANES, LANES), LANES)
    theirs = pl.ds(pl.multiple_of(LANES - core * LANES, LANES), LANES)

    def enc_pair():
        return (
            remote(enc.at[0], WE.at[:, mine], w_s.at[0], w_r.at[0], partner),
            remote(bias, BE.at[:, mine], w_s.at[1], w_r.at[1], partner),
        )

    def enc_local():
        return (
            pltpu.make_async_copy(enc.at[0], WE.at[:, mine], loc_sem.at[0]),
            pltpu.make_async_copy(bias, BE.at[:, mine], loc_sem.at[1]),
        )

    def dec_remote(s):
        return remote(dec.at[0, s], WD.at[s, mine, :], d_s.at[s], d_r.at[s], partner)

    def dec_arrive(s):
        slot = WD.at[s, theirs, :]
        remote(slot, slot, d_s.at[s], d_r.at[s], partner).wait_recv()

    def dec_local(s):
        return pltpu.make_async_copy(dec.at[0, s], WD.at[s, mine, :], dloc_sem.at[s])

    def own_rows(q):
        return pltpu.make_async_copy(resid.at[0, pl.ds(q * ROWS, ROWS), :], R.at[q, x, y], own_sem.at[q])

    mlp_copy = pltpu.make_async_copy(mlp.at[0], MV, loc_sem.at[2])

    def encode(q):
        if q == 0:
            for copy in enc_local():
                copy.wait()
            for slot, k in ((WE.at[:, theirs], 0), (BE.at[:, theirs], 1)):
                remote(slot, slot, w_s.at[k], w_r.at[k], partner).wait_recv()
        rows = R[q].reshape(SIDE * SIDE * ROWS, D)
        pre = jnp.dot(rows, WE[...], preferred_element_type=jnp.float32) + BE[...]
        L[q, z] = jnp.maximum(pre, 0.0).astype(jnp.bfloat16)

    def z_forward(q, i):
        s = lax.rem(z + LAYERS - i, LAYERS)
        return remote(L.at[q, s], L.at[q, s], zf_s.at[q, i], zf_r.at[q, i], at_layer(up))

    def forward_sends(i):
        return jnp.logical_and(z >= i, z < LAYERS - 1)

    def z_backward(q, i):
        s = lax.rem(z + i, LAYERS)
        return remote(L.at[q, s], L.at[q, s], zb_s.at[q, i], zb_r.at[q, i], at_layer(down))

    def backward_sends(i):
        return lax.rem(z + i, LAYERS) < BACKWARD

    def z_send(q, i):
        if i < FORWARD:
            @pl.when(forward_sends(i))
            def _():
                z_forward(q, i).start()
        if i < BACKWARD:
            @pl.when(backward_sends(i))
            def _():
                z_backward(q, i).start()

    def z_arrive(q, i):
        if i < FORWARD:
            @pl.when(z >= i + 1)
            def _():
                slot = L.at[q, lax.rem(z + LAYERS - 1 - i, LAYERS)]
                remote(slot, slot, zf_s.at[q, i], zf_r.at[q, i], partner).wait_recv()
        if i < BACKWARD:
            @pl.when(lax.rem(z + 1 + i, LAYERS) < BACKWARD)
            def _():
                slot = L.at[q, lax.rem(z + 1 + i, LAYERS)]
                remote(slot, slot, zb_s.at[q, i], zb_r.at[q, i], partner).wait_recv()

    def add(q, s, first):
        def tile(n, carry):
            cols = pl.ds(pl.multiple_of(n * TILE, TILE), TILE)
            part = jnp.dot(L[q, s], WD[s, :, cols], preferred_element_type=jnp.float32)
            part = part.reshape(SIDE, SIDE, ROWS, TILE)
            if first:
                ACC[q, :, :, :, cols] = part
            else:
                ACC[q, :, :, :, cols] += part
            return carry

        lax.fori_loop(0, D // TILE, tile, 0)

    def z_add(q, i):
        if i < FORWARD:
            @pl.when(z >= i + 1)
            def _():
                add(q, lax.rem(z + LAYERS - 1 - i, LAYERS), False)
        if i < BACKWARD:
            source = lax.rem(z + 1 + i, LAYERS)

            @pl.when(jnp.logical_and(source < BACKWARD, source < z))
            def _():
                add(q, source, False)

    def z_step(q, i):
        z_arrive(q, i)
        z_send(q, i + 1)
        z_add(q, i)

    def rs1(q, h, j):
        cols = pl.ds(h * HALF, HALF)
        o = OFFSETS[j]
        if h == 0:
            return remote(S.at[q, move(x, o), :, :, cols], TA.at[q, j], rs1_s.at[q, h, j], rs1_r.at[q, h, j], at_chip(move(x, o), y))
        return remote(S.at[q, :, move(y, o), :, cols], TB.at[q, j], rs1_s.at[q, h, j], rs1_r.at[q, h, j], at_chip(x, move(y, o)))

    def rs1_start(q):
        def tile(n, carry):
            cols = pl.ds(pl.multiple_of(n * TILE, TILE), TILE)
            S[q, :, :, :, cols] = ACC[q, :, :, :, cols].astype(jnp.bfloat16)
            return carry

        lax.fori_loop(0, D // TILE, tile, 0)
        for j in (2, 0, 1):
            for h in range(2):
                rs1(q, h, j).start()

    def rs2(q, h, j):
        o = OFFSETS[j]
        if h == 0:
            return remote(VA.at[q, move(y, o)], UA.at[q, j], rs2_s.at[q, h, j], rs2_r.at[q, h, j], at_chip(x, move(y, o)))
        return remote(VB.at[q, move(x, o)], UB.at[q, j], rs2_s.at[q, h, j], rs2_r.at[q, h, j], at_chip(move(x, o), y))

    def rs2_start(q):
        for h, T, V in ((0, TA, VA), (1, TB, VB)):
            cols = pl.ds(h * HALF, HALF)
            for j in (0, 1, 2):
                slot = T.at[q, j]
                remote(slot, slot, rs1_s.at[q, h, j], rs1_r.at[q, h, j], partner).wait_recv()

            def line(k, carry):
                at = (q, x, k, slice(None), cols) if h == 0 else (q, k, y, slice(None), cols)
                total = ACC[at]
                for j in range(3):
                    total = total + T[q, j, k].astype(jnp.float32)
                ACC[at] = total
                V[q, k] = total.astype(jnp.bfloat16)
                return carry

            lax.fori_loop(0, SIDE, line, 0)
            for j in (2, 0, 1):
                rs2(q, h, j).start()

    def finish(q):
        if q == 0:
            mlp_copy.wait()
        rows = pl.ds(q * ROWS, ROWS)
        for h, U in ((0, UA), (1, UB)):
            cols = pl.ds(h * HALF, HALF)
            for j in (0, 1, 2):
                slot = U.at[q, j]
                remote(slot, slot, rs2_s.at[q, h, j], rs2_r.at[q, h, j], partner).wait_recv()
            total = ACC[q, x, y, :, cols]
            for j in range(3):
                total = total + U[q, j].astype(jnp.float32)
            OV[rows, cols] = (MV[rows, cols].astype(jnp.float32) - total).astype(jnp.bfloat16)
        pltpu.make_async_copy(OV.at[rows, :], out.at[0, rows, :], out_sem.at[q]).start()

    ag1_start(0)
    for copy in enc_pair():
        copy.start()
    ag1_start(1)
    own_rows(0).start()
    for copy in enc_local():
        copy.start()
    own_rows(1).start()

    def weights(s, carry):
        dec_remote(s).start()
        dec_local(s).start()
        return carry

    lax.fori_loop(0, z + 1, weights, 0)
    mlp_copy.start()

    for h in range(2):
        ag1_wait(0, h)
    own_rows(0).wait()
    for h in range(2):
        ag2_start(0, h)
    ag2_relay(0)
    for h in range(2):
        ag1_wait(1, h)
    own_rows(1).wait()
    for h in range(2):
        ag2_start(1, h)
    ag2_rest(0)
    encode(0)
    z_send(0, 0)
    ag2_relay(1)

    def ready(s, carry):
        dec_arrive(s)
        dec_local(s).wait()
        return carry

    lax.fori_loop(0, z + 1, ready, 0)
    add(0, z, True)
    z_step(0, 0)
    ag2_rest(1)
    encode(1)
    z_send(1, 0)
    add(1, z, True)
    z_step(0, 1)
    z_step(1, 0)
    z_step(0, 2)
    z_step(1, 1)
    z_step(0, 3)
    rs1_start(0)
    z_step(1, 2)
    z_step(1, 3)
    rs1_start(1)
    rs2_start(0)
    finish(0)
    rs2_start(1)
    finish(1)

    for q in range(CHUNKS):
        rows = pl.ds(q * ROWS, ROWS)
        for h in range(2):
            for j in range(3):
                ag1(q, h, j).wait_send()
                rs1(q, h, j).wait_send()
                rs2(q, h, j).wait_send()
            for direction in range(2):
                for piece in range(3):
                    ag2(q, h, direction, piece).wait_send()
        for i in range(FORWARD):
            @pl.when(forward_sends(i))
            def _():
                z_forward(q, i).wait_send()
        for i in range(BACKWARD):
            @pl.when(backward_sends(i))
            def _():
                z_backward(q, i).wait_send()
        pltpu.make_async_copy(OV.at[rows, :], out.at[0, rows, :], out_sem.at[q]).wait()
    for copy in enc_pair():
        copy.wait_send()

    def drained(s, carry):
        dec_remote(s).wait_send()
        return carry

    lax.fori_loop(0, z + 1, drained, 0)


def body(*args):
    bf16, f32 = jnp.bfloat16, jnp.float32
    dma = pltpu.SemaphoreType.DMA
    any_space = pl.BlockSpec(memory_space=pl.ANY)
    block = (CHUNKS, SIDE, SIDE, ROWS, D)
    return pl.pallas_call(
        kernel,
        out_shape=jax.ShapeDtypeStruct(args[0].shape, bf16),
        in_specs=[any_space] * 5,
        out_specs=any_space,
        scratch_shapes=[
            pltpu.VMEM(block, bf16),
            pltpu.VMEM((D, 2 * LANES), bf16),
            pltpu.VMEM((1, 2 * LANES), f32),
            pltpu.VMEM((LAYERS, 2 * LANES, D), bf16),
            pltpu.VMEM((CHUNKS, LAYERS, SIDE * SIDE * ROWS, 2 * LANES), bf16),
            pltpu.VMEM(block, f32),
            pltpu.VMEM(block, bf16),
            pltpu.VMEM((CHUNKS, 3, SIDE, ROWS, HALF), bf16),
            pltpu.VMEM((CHUNKS, 3, SIDE, ROWS, HALF), bf16),
            pltpu.VMEM((CHUNKS, SIDE, ROWS, HALF), bf16),
            pltpu.VMEM((CHUNKS, SIDE, ROWS, HALF), bf16),
            pltpu.VMEM((CHUNKS, 3, ROWS, HALF), bf16),
            pltpu.VMEM((CHUNKS, 3, ROWS, HALF), bf16),
            pltpu.VMEM((CHUNKS * ROWS, D), bf16),
            pltpu.VMEM((CHUNKS * ROWS, D), bf16),
            dma((CHUNKS, 2, 3)), dma((CHUNKS, 2, 3)),
            dma((CHUNKS, 2, 2, 3)), dma((CHUNKS, 2, 2, 3)),
            dma((2,)), dma((2,)),
            dma((LAYERS,)), dma((LAYERS,)),
            dma((CHUNKS, FORWARD)), dma((CHUNKS, FORWARD)),
            dma((CHUNKS, BACKWARD)), dma((CHUNKS, BACKWARD)),
            dma((CHUNKS, 2, 3)), dma((CHUNKS, 2, 3)),
            dma((CHUNKS, 2, 3)), dma((CHUNKS, 2, 3)),
            dma((CHUNKS,)), dma((3,)), dma((LAYERS,)), dma((CHUNKS,)),
        ],
        compiler_params=pltpu.CompilerParams(
            collective_id=0, has_side_effects=True, vmem_limit_bytes=60 * 2**20
        ),
    )(*args)


def solution(mesh):
    return jax.shard_map(
        body,
        mesh=mesh,
        in_specs=(
            P("layer", "latent", None),
            P("layer", "latent", None),
            P("layer", None, "latent"),
            P("layer", "latent"),
            P("layer", None, "latent", None),
        ),
        out_specs=P("layer", "latent", None),
        check_vma=False,
    )
```

```python
import functools

import jax
import jax.numpy as jnp
from jax import lax
from jax.experimental import pallas as pl
from jax.experimental.pallas import tpu as pltpu
from jax.sharding import PartitionSpec as P

MESH = pl.DeviceIdType.MESH
LAYERS = 8
SIDE = 4
CHUNKS = 4
ROWS = 8
D = 4096
HALF = 2048
QUARTER = 1024
LANES = 128
TILE = 2048
OFFSETS = (1, SIDE - 1, 2)
FORWARD = 4
BACKWARD = 3

SCHEDULE = (
    ("first", 0), ("start", 0), ("first", 1), ("first", 2), ("first", 3), ("second", 0),
    ("second", 1), ("relay", 0), ("second", 2), ("relay", 1), ("second", 3),
    ("code", 0), ("send", 0), ("relay", 2), ("own", 0), ("z0", 0), ("code", 1),
    ("send", 1), ("relay", 3), ("own", 1), ("z1", 0), ("z0", 1), ("code", 2), ("z2", 0),
    ("send", 2), ("own", 2), ("z1", 1), ("code", 3), ("own", 3), ("z3", 0), ("rs1", 0),
    ("z0", 2), ("z2", 1), ("send", 3), ("z1", 2), ("add", 0), ("z3", 1), ("rs1", 1),
    ("z0", 3), ("z2", 2), ("rs2", 0), ("z1", 3), ("add", 1), ("z3", 2), ("rs1", 2),
    ("end", 0), ("z2", 3), ("rs2", 1), ("add", 2), ("z3", 3), ("rs1", 3), ("end", 1),
    ("rs2", 2), ("add", 3), ("end", 2), ("rs2", 3), ("end", 3),
)


def kernel(
    resid, mlp, enc, bias, dec, out,
    R, WE, BE, WD, L, ACC, S, FA, FB, TA, TB, VA, VB, UA, UB, MV, OV,
    ag1_s, ag1_r, ag2_s, ag2_r, w_s, w_r, d_s, d_r, zf_s, zf_r, zb_s, zb_r,
    rs1_s, rs1_r, rs2_s, rs2_r, own_sem, mlp_sem, loc_sem, dloc_sem, out_sem,
):
    z = lax.axis_index("layer")
    index = lax.axis_index("latent")
    core = lax.rem(index, 2)
    y = lax.rem(lax.div(index, 2), SIDE)
    x = lax.div(index, 2 * SIDE)

    def at_chip(px, py):
        return {"layer": z, "latent": (px * SIDE + py) * 2 + core}

    def at_layer(pz):
        return {"layer": pz, "latent": index}

    partner = {"layer": z, "latent": index + 1 - 2 * core}

    def move(v, o):
        return lax.rem(v + o, SIDE)

    def remote(src, dst, ss, rs, where):
        return pltpu.make_async_remote_copy(
            src_ref=src, dst_ref=dst, send_sem=ss, recv_sem=rs,
            device_id=where, device_id_type=MESH,
        )

    up, down = lax.rem(z + 1, LAYERS), lax.rem(z + LAYERS - 1, LAYERS)

    barrier = pltpu.get_barrier_semaphore()
    friends = [partner, at_layer(up), at_layer(down)]
    friends += [at_chip(move(x, o), y) for o in OFFSETS]
    friends += [at_chip(x, move(y, o)) for o in OFFSETS]
    for friend in friends:
        pl.semaphore_signal(barrier, inc=1, device_id=friend, device_id_type=MESH)
    pl.semaphore_wait(barrier, len(friends))

    def ag1(q, h, j):
        cols = pl.ds(h * HALF, HALF)
        o = OFFSETS[j]
        where = at_chip(move(x, o), y) if h == 0 else at_chip(x, move(y, o))
        return remote(
            resid.at[0, pl.ds(q * ROWS, ROWS), cols], R.at[q, x, y, :, cols],
            ag1_s.at[q, h, j], ag1_r.at[q, h, j], where,
        )

    def ag1_start(q):
        for j in range(3):
            for h in range(2):
                ag1(q, h, j).start()

    def ag1_wait(q, h):
        cols = pl.ds(h * HALF, HALF)
        for j in range(3):
            back = SIDE - OFFSETS[j]
            slot = R.at[q, move(x, back), y, :, cols] if h == 0 else R.at[q, x, move(y, back), :, cols]
            remote(slot, slot, ag1_s.at[q, h, j], ag1_r.at[q, h, j], partner).wait_recv()

    def lines(q, h, back, cols):
        if h == 0:
            return R.at[q, :, move(y, back), :, cols]
        return R.at[q, move(x, back), :, :, cols]

    def ag2(q, h, direction, piece):
        step = 1 if direction == 0 else SIDE - 1
        first = direction if piece != 1 else 1 - direction
        cols = pl.ds(h * HALF + first * QUARTER, QUARTER)
        back = 0 if piece < 2 else SIDE - step
        where = at_chip(x, move(y, step)) if h == 0 else at_chip(move(x, step), y)
        block = lines(q, h, back, cols)
        return remote(block, block, ag2_s.at[q, h, direction, piece], ag2_r.at[q, h, direction, piece], where)

    def ag2_arrive(q, h, direction, piece):
        step = 1 if direction == 0 else SIDE - 1
        first = direction if piece != 1 else 1 - direction
        cols = pl.ds(h * HALF + first * QUARTER, QUARTER)
        back = SIDE - step if piece < 2 else 2
        block = lines(q, h, back, cols)
        remote(block, block, ag2_s.at[q, h, direction, piece], ag2_r.at[q, h, direction, piece], partner).wait_recv()

    def ag2_start(q, h):
        for piece in range(2):
            for direction in range(2):
                ag2(q, h, direction, piece).start()

    def ag2_relay(q):
        for h in range(2):
            for direction in range(2):
                ag2_arrive(q, h, direction, 0)
                ag2(q, h, direction, 2).start()

    def ag2_rest(q):
        for piece in (1, 2):
            for h in range(2):
                for direction in range(2):
                    ag2_arrive(q, h, direction, piece)

    mine = pl.ds(pl.multiple_of(core * LANES, LANES), LANES)
    theirs = pl.ds(pl.multiple_of(LANES - core * LANES, LANES), LANES)

    def enc_pair():
        return (
            remote(enc.at[0], WE.at[:, mine], w_s.at[0], w_r.at[0], partner),
            remote(bias, BE.at[:, mine], w_s.at[1], w_r.at[1], partner),
        )

    def enc_local():
        return (
            pltpu.make_async_copy(enc.at[0], WE.at[:, mine], loc_sem.at[0]),
            pltpu.make_async_copy(bias, BE.at[:, mine], loc_sem.at[1]),
        )

    def dec_remote(s):
        return remote(dec.at[0, s], WD.at[s, mine, :], d_s.at[s], d_r.at[s], partner)

    def dec_arrive(s):
        slot = WD.at[s, theirs, :]
        remote(slot, slot, d_s.at[s], d_r.at[s], partner).wait_recv()

    def dec_local(s):
        return pltpu.make_async_copy(dec.at[0, s], WD.at[s, mine, :], dloc_sem.at[s])

    def own_rows(q):
        return pltpu.make_async_copy(resid.at[0, pl.ds(q * ROWS, ROWS), :], R.at[q, x, y], own_sem.at[q])

    def mlp_copy(q):
        return pltpu.make_async_copy(mlp.at[0, pl.ds(q * ROWS, ROWS), :], MV.at[q], mlp_sem.at[q])

    def encode(q):
        if q == 0:
            for copy in enc_local():
                copy.wait()
            for slot, k in ((WE.at[:, theirs], 0), (BE.at[:, theirs], 1)):
                remote(slot, slot, w_s.at[k], w_r.at[k], partner).wait_recv()
        rows = R[q].reshape(SIDE * SIDE * ROWS, D)
        pre = jnp.dot(rows, WE[...], preferred_element_type=jnp.float32) + BE[...]
        L[q, z] = jnp.maximum(pre, 0.0).astype(jnp.bfloat16)

    def z_forward(q, i):
        s = lax.rem(z + LAYERS - i, LAYERS)
        return remote(L.at[q, s], L.at[q, s], zf_s.at[q, i], zf_r.at[q, i], at_layer(up))

    def forward_sends(i):
        return jnp.logical_and(z >= i, z < LAYERS - 1)

    def z_backward(q, i):
        s = lax.rem(z + i, LAYERS)
        return remote(L.at[q, s], L.at[q, s], zb_s.at[q, i], zb_r.at[q, i], at_layer(down))

    def backward_sends(i):
        return lax.rem(z + i, LAYERS) < BACKWARD

    def z_send(q, i):
        if i < FORWARD:
            @pl.when(forward_sends(i))
            def _():
                z_forward(q, i).start()
        if i < BACKWARD:
            @pl.when(backward_sends(i))
            def _():
                z_backward(q, i).start()

    def z_arrive(q, i):
        if i < FORWARD:
            @pl.when(z >= i + 1)
            def _():
                slot = L.at[q, lax.rem(z + LAYERS - 1 - i, LAYERS)]
                remote(slot, slot, zf_s.at[q, i], zf_r.at[q, i], partner).wait_recv()
        if i < BACKWARD:
            @pl.when(lax.rem(z + 1 + i, LAYERS) < BACKWARD)
            def _():
                slot = L.at[q, lax.rem(z + 1 + i, LAYERS)]
                remote(slot, slot, zb_s.at[q, i], zb_r.at[q, i], partner).wait_recv()

    def add(q, s, first):
        if q == 0:
            dec_arrive(s)
            dec_local(s).wait()

        def tile(n, carry):
            cols = pl.ds(pl.multiple_of(n * TILE, TILE), TILE)
            part = jnp.dot(L[q, s], WD[s, :, cols], preferred_element_type=jnp.float32)
            part = part.reshape(SIDE, SIDE, ROWS, TILE)
            if first:
                ACC[q, :, :, :, cols] = part
            else:
                ACC[q, :, :, :, cols] += part
            return carry

        lax.fori_loop(0, D // TILE, tile, 0)

    def z_add(q, i):
        if i < FORWARD:
            @pl.when(z >= i + 1)
            def _():
                add(q, lax.rem(z + LAYERS - 1 - i, LAYERS), False)
        if i < BACKWARD:
            source = lax.rem(z + 1 + i, LAYERS)

            @pl.when(jnp.logical_and(source < BACKWARD, source < z))
            def _():
                add(q, source, False)

    def z_step(q, i):
        z_arrive(q, i)
        z_send(q, i + 1)
        z_add(q, i)

    def line_of(h, offset):
        return move(x, offset) if h == 0 else move(y, offset)

    def place(q, h, k, cols):
        return (q, k, slice(None), slice(None), cols) if h == 0 else (q, slice(None), k, slice(None), cols)

    def neighbour(h, offset):
        return at_chip(move(x, offset), y) if h == 0 else at_chip(x, move(y, offset))

    def rs1(q, h, direction, piece):
        step = 1 if direction == 0 else SIDE - 1
        quarter = direction if piece != 1 else 1 - direction
        cols = pl.ds(h * HALF + quarter * QUARTER, QUARTER)
        src = S.at[place(q, h, line_of(h, 2 if piece == 0 else step), cols)]
        dst = (FA, FB)[h].at[q, direction] if piece == 0 else (TA, TB)[h].at[q, direction, :, :, pl.ds(quarter * QUARTER, QUARTER)]
        return remote(src, dst, rs1_s.at[q, h, direction, piece], rs1_r.at[q, h, direction, piece], neighbour(h, step))

    def rs1_arrive(q, h, direction, piece):
        quarter = direction if piece != 1 else 1 - direction
        slot = (FA, FB)[h].at[q, direction] if piece == 0 else (TA, TB)[h].at[q, direction, :, :, pl.ds(quarter * QUARTER, QUARTER)]
        remote(slot, slot, rs1_s.at[q, h, direction, piece], rs1_r.at[q, h, direction, piece], partner).wait_recv()

    def rs1_start(q):
        def tile(n, carry):
            cols = pl.ds(pl.multiple_of(n * TILE, TILE), TILE)
            S[q, :, :, :, cols] = ACC[q, :, :, :, cols].astype(jnp.bfloat16)
            return carry

        lax.fori_loop(0, D // TILE, tile, 0)
        for piece in range(2):
            for h in range(2):
                for direction in range(2):
                    rs1(q, h, direction, piece).start()

    def rs1_relay(q):
        for h in range(2):
            for direction in range(2):
                step = 1 if direction == 0 else SIDE - 1
                rs1_arrive(q, h, direction, 0)
                at = place(q, h, line_of(h, step), pl.ds(h * HALF + direction * QUARTER, QUARTER))
                far = (FA, FB)[h][q, direction].astype(jnp.float32)
                S[at] = (ACC[at] + far).astype(jnp.bfloat16)
                rs1(q, h, direction, 2).start()

    def rs2(q, h, j):
        o = OFFSETS[j]
        if h == 0:
            return remote(VA.at[q, move(y, o)], UA.at[q, j], rs2_s.at[q, h, j], rs2_r.at[q, h, j], at_chip(x, move(y, o)))
        return remote(VB.at[q, move(x, o)], UB.at[q, j], rs2_s.at[q, h, j], rs2_r.at[q, h, j], at_chip(move(x, o), y))

    def rs2_start(q):
        for h, T, V in ((0, TA, VA), (1, TB, VB)):
            cols = pl.ds(h * HALF, HALF)
            for piece in (1, 2):
                for direction in range(2):
                    rs1_arrive(q, h, direction, piece)

            def line(k, carry):
                at = (q, x, k, slice(None), cols) if h == 0 else (q, k, y, slice(None), cols)
                total = ACC[at]
                for j in range(2):
                    total = total + T[q, j, k].astype(jnp.float32)
                ACC[at] = total
                V[q, k] = total.astype(jnp.bfloat16)
                return carry

            lax.fori_loop(0, SIDE, line, 0)
            for j in (2, 0, 1):
                rs2(q, h, j).start()

    def result(q):
        return pltpu.make_async_copy(OV.at[q], out.at[0, pl.ds(q * ROWS, ROWS), :], out_sem.at[q])

    def finish(q):
        mlp_copy(q).wait()
        for h, U in ((0, UA), (1, UB)):
            cols = pl.ds(h * HALF, HALF)
            for j in (0, 1, 2):
                slot = U.at[q, j]
                remote(slot, slot, rs2_s.at[q, h, j], rs2_r.at[q, h, j], partner).wait_recv()
            total = ACC[q, x, y, :, cols]
            for j in range(3):
                total = total + U[q, j].astype(jnp.float32)
            OV[q, :, cols] = (MV[q, :, cols].astype(jnp.float32) - total).astype(jnp.bfloat16)
        result(q).start()

    def weights(k, carry):
        dec_remote(z - k).start()
        dec_local(z - k).start()
        return carry

    def start(q):
        for copy in enc_pair():
            copy.start()
        for copy in enc_local():
            copy.start()
        for c in range(CHUNKS):
            own_rows(c).start()
        lax.fori_loop(0, z + 1, weights, 0)
        for c in range(CHUNKS):
            mlp_copy(c).start()

    def second(q):
        own_rows(q).wait()
        for h in range(2):
            ag1_wait(q, h)
        for h in range(2):
            ag2_start(q, h)

    def code(q):
        ag2_rest(q)
        encode(q)

    def send(q):
        z_send(q, 0)

    def own(q):
        add(q, z, True)

    steps = {
        "first": ag1_start, "start": start, "second": second, "relay": ag2_relay,
        "code": code, "send": send, "own": own, "rs1": rs1_start, "add": rs1_relay, "rs2": rs2_start, "end": finish,
    }
    for name, q in SCHEDULE:
        if name[0] == "z":
            z_step(q, int(name[1]))
        else:
            steps[name](q)

    for q in range(CHUNKS):
        for h in range(2):
            for j in range(3):
                ag1(q, h, j).wait_send()
                rs2(q, h, j).wait_send()
            for direction in range(2):
                for piece in range(3):
                    ag2(q, h, direction, piece).wait_send()
                    rs1(q, h, direction, piece).wait_send()
        for i in range(FORWARD):
            @pl.when(forward_sends(i))
            def _():
                z_forward(q, i).wait_send()
        for i in range(BACKWARD):
            @pl.when(backward_sends(i))
            def _():
                z_backward(q, i).wait_send()
        result(q).wait()
    for copy in enc_pair():
        copy.wait_send()

    def drained(s, carry):
        dec_remote(s).wait_send()
        return carry

    lax.fori_loop(0, z + 1, drained, 0)


def body(*args):
    bf16, f32 = jnp.bfloat16, jnp.float32
    dma = pltpu.SemaphoreType.DMA
    any_space = pl.BlockSpec(memory_space=pl.ANY)
    block = (CHUNKS, SIDE, SIDE, ROWS, D)
    return pl.pallas_call(
        kernel,
        out_shape=jax.ShapeDtypeStruct(args[0].shape, bf16),
        in_specs=[any_space] * 5,
        out_specs=any_space,
        scratch_shapes=[
            pltpu.VMEM(block, bf16),
            pltpu.VMEM((D, 2 * LANES), bf16),
            pltpu.VMEM((1, 2 * LANES), f32),
            pltpu.VMEM((LAYERS, 2 * LANES, D), bf16),
            pltpu.VMEM((CHUNKS, LAYERS, SIDE * SIDE * ROWS, 2 * LANES), bf16),
            pltpu.VMEM(block, f32),
            pltpu.VMEM(block, bf16),
            pltpu.VMEM((CHUNKS, 2, SIDE, ROWS, QUARTER), bf16),
            pltpu.VMEM((CHUNKS, 2, SIDE, ROWS, QUARTER), bf16),
            pltpu.VMEM((CHUNKS, 2, SIDE, ROWS, HALF), bf16),
            pltpu.VMEM((CHUNKS, 2, SIDE, ROWS, HALF), bf16),
            pltpu.VMEM((CHUNKS, SIDE, ROWS, HALF), bf16),
            pltpu.VMEM((CHUNKS, SIDE, ROWS, HALF), bf16),
            pltpu.VMEM((CHUNKS, 3, ROWS, HALF), bf16),
            pltpu.VMEM((CHUNKS, 3, ROWS, HALF), bf16),
            pltpu.VMEM((CHUNKS, ROWS, D), bf16),
            pltpu.VMEM((CHUNKS, ROWS, D), bf16),
            dma((CHUNKS, 2, 3)), dma((CHUNKS, 2, 3)),
            dma((CHUNKS, 2, 2, 3)), dma((CHUNKS, 2, 2, 3)),
            dma((2,)), dma((2,)),
            dma((LAYERS,)), dma((LAYERS,)),
            dma((CHUNKS, FORWARD)), dma((CHUNKS, FORWARD)),
            dma((CHUNKS, BACKWARD)), dma((CHUNKS, BACKWARD)),
            dma((CHUNKS, 2, 2, 3)), dma((CHUNKS, 2, 2, 3)),
            dma((CHUNKS, 2, 3)), dma((CHUNKS, 2, 3)),
            dma((CHUNKS,)), dma((CHUNKS,)), dma((2,)), dma((LAYERS,)), dma((CHUNKS,)),
        ],
        compiler_params=pltpu.CompilerParams(
            collective_id=0, has_side_effects=True, vmem_limit_bytes=60 * 2**20
        ),
    )(*args)


def solution(mesh):
    return jax.shard_map(
        body,
        mesh=mesh,
        in_specs=(
            P("layer", "latent", None),
            P("layer", "latent", None),
            P("layer", None, "latent"),
            P("layer", "latent"),
            P("layer", None, "latent", None),
        ),
        out_specs=P("layer", "latent", None),
        check_vma=False,
    )
```

```python
import functools

import jax
import jax.numpy as jnp
from jax import lax
from jax.experimental import pallas as pl
from jax.experimental.pallas import tpu as pltpu
from jax.sharding import PartitionSpec as P

MESH = pl.DeviceIdType.MESH
LAYERS = 8
SIDE = 4
CHUNKS = 4
ROWS = 8
D = 4096
HALF = 2048
QUARTER = 1024
LANES = 128
TILE = 4096
OFFSETS = (1, SIDE - 1, 2)
FORWARD = 4
BACKWARD = 3

SCHEDULE = (
    ("first", 0), ("start", 0), ("first", 1), ("first", 2), ("first", 3), ("second", 0),
    ("second", 1), ("relay", 0), ("second", 2), ("relay", 1), ("second", 3),
    ("code", 0), ("send", 0), ("relay", 2), ("own", 0), ("z0", 0), ("code", 1),
    ("send", 1), ("relay", 3), ("own", 1), ("z1", 0), ("z0", 1), ("code", 2), ("z2", 0),
    ("send", 2), ("own", 2), ("z1", 1), ("code", 3), ("own", 3), ("z3", 0), ("rs1", 0),
    ("z0", 2), ("z2", 1), ("send", 3), ("z1", 2), ("add", 0), ("z3", 1), ("rs1", 1),
    ("z0", 3), ("z2", 2), ("rs2", 0), ("z1", 3), ("add", 1), ("z3", 2), ("rs1", 2),
    ("end", 0), ("z2", 3), ("rs2", 1), ("add", 2), ("z3", 3), ("rs1", 3), ("end", 1),
    ("rs2", 2), ("add", 3), ("end", 2), ("rs2", 3), ("end", 3),
)


def kernel(
    resid, mlp, enc, bias, dec, out,
    R, WE, BE, WD, L, ACC, S, FA, FB, TA, TB, VA, VB, UA, UB, MV, OV,
    ag1_s, ag1_r, ag2_s, ag2_r, w_s, w_r, d_s, d_r, zf_s, zf_r, zb_s, zb_r,
    rs1_s, rs1_r, rs2_s, rs2_r, own_sem, mlp_sem, loc_sem, dloc_sem, out_sem,
):
    z = lax.axis_index("layer")
    index = lax.axis_index("latent")
    core = lax.rem(index, 2)
    y = lax.rem(lax.div(index, 2), SIDE)
    x = lax.div(index, 2 * SIDE)

    def at_chip(px, py):
        return {"layer": z, "latent": (px * SIDE + py) * 2 + core}

    def at_layer(pz):
        return {"layer": pz, "latent": index}

    partner = {"layer": z, "latent": index + 1 - 2 * core}

    def move(v, o):
        return lax.rem(v + o, SIDE)

    def remote(src, dst, ss, rs, where):
        return pltpu.make_async_remote_copy(
            src_ref=src, dst_ref=dst, send_sem=ss, recv_sem=rs,
            device_id=where, device_id_type=MESH,
        )

    up, down = lax.rem(z + 1, LAYERS), lax.rem(z + LAYERS - 1, LAYERS)

    barrier = pltpu.get_barrier_semaphore()
    friends = [partner, at_layer(up), at_layer(down)]
    friends += [at_chip(move(x, o), y) for o in OFFSETS]
    friends += [at_chip(x, move(y, o)) for o in OFFSETS]
    for friend in friends:
        pl.semaphore_signal(barrier, inc=1, device_id=friend, device_id_type=MESH)
    pl.semaphore_wait(barrier, len(friends))

    def ag1(q, h, j):
        cols = pl.ds(h * HALF, HALF)
        o = OFFSETS[j]
        where = at_chip(move(x, o), y) if h == 0 else at_chip(x, move(y, o))
        return remote(
            resid.at[0, pl.ds(q * ROWS, ROWS), cols], R.at[q, x, y, :, cols],
            ag1_s.at[q, h, j], ag1_r.at[q, h, j], where,
        )

    def ag1_start(q):
        for j in (2, 0, 1):
            for h in range(2):
                ag1(q, h, j).start()

    def ag1_wait(q, h):
        cols = pl.ds(h * HALF, HALF)
        for j in range(3):
            back = SIDE - OFFSETS[j]
            slot = R.at[q, move(x, back), y, :, cols] if h == 0 else R.at[q, x, move(y, back), :, cols]
            remote(slot, slot, ag1_s.at[q, h, j], ag1_r.at[q, h, j], partner).wait_recv()

    def lines(q, h, back, cols):
        if h == 0:
            return R.at[q, :, move(y, back), :, cols]
        return R.at[q, move(x, back), :, :, cols]

    def ag2(q, h, direction, piece):
        step = 1 if direction == 0 else SIDE - 1
        first = direction if piece != 1 else 1 - direction
        cols = pl.ds(h * HALF + first * QUARTER, QUARTER)
        back = 0 if piece < 2 else SIDE - step
        where = at_chip(x, move(y, step)) if h == 0 else at_chip(move(x, step), y)
        block = lines(q, h, back, cols)
        return remote(block, block, ag2_s.at[q, h, direction, piece], ag2_r.at[q, h, direction, piece], where)

    def ag2_arrive(q, h, direction, piece):
        step = 1 if direction == 0 else SIDE - 1
        first = direction if piece != 1 else 1 - direction
        cols = pl.ds(h * HALF + first * QUARTER, QUARTER)
        back = SIDE - step if piece < 2 else 2
        block = lines(q, h, back, cols)
        remote(block, block, ag2_s.at[q, h, direction, piece], ag2_r.at[q, h, direction, piece], partner).wait_recv()

    def ag2_start(q, h):
        for piece in range(2):
            for direction in range(2):
                ag2(q, h, direction, piece).start()

    def ag2_relay(q):
        for h in range(2):
            for direction in range(2):
                ag2_arrive(q, h, direction, 0)
                ag2(q, h, direction, 2).start()

    def ag2_rest(q):
        for piece in (1, 2):
            for h in range(2):
                for direction in range(2):
                    ag2_arrive(q, h, direction, piece)

    mine = pl.ds(pl.multiple_of(core * LANES, LANES), LANES)
    theirs = pl.ds(pl.multiple_of(LANES - core * LANES, LANES), LANES)

    def enc_pair():
        return (
            remote(enc.at[0], WE.at[:, mine], w_s.at[0], w_r.at[0], partner),
            remote(bias, BE.at[:, mine], w_s.at[1], w_r.at[1], partner),
        )

    def enc_local():
        return (
            pltpu.make_async_copy(enc.at[0], WE.at[:, mine], loc_sem.at[0]),
            pltpu.make_async_copy(bias, BE.at[:, mine], loc_sem.at[1]),
        )

    def dec_remote(s):
        return remote(dec.at[0, s], WD.at[s, mine, :], d_s.at[s], d_r.at[s], partner)

    def dec_arrive(s):
        slot = WD.at[s, theirs, :]
        remote(slot, slot, d_s.at[s], d_r.at[s], partner).wait_recv()

    def dec_local(s):
        return pltpu.make_async_copy(dec.at[0, s], WD.at[s, mine, :], dloc_sem.at[s])

    def own_rows(q):
        return pltpu.make_async_copy(resid.at[0, pl.ds(q * ROWS, ROWS), :], R.at[q, x, y], own_sem.at[q])

    def mlp_copy(q):
        return pltpu.make_async_copy(mlp.at[0, pl.ds(q * ROWS, ROWS), :], MV.at[q], mlp_sem.at[q])

    def encode(q):
        if q == 0:
            for copy in enc_local():
                copy.wait()
            for slot, k in ((WE.at[:, theirs], 0), (BE.at[:, theirs], 1)):
                remote(slot, slot, w_s.at[k], w_r.at[k], partner).wait_recv()
        rows = R[q].reshape(SIDE * SIDE * ROWS, D)
        pre = jnp.dot(rows, WE[...], preferred_element_type=jnp.float32) + BE[...]
        L[q, z] = jnp.maximum(pre, 0.0).astype(jnp.bfloat16)

    def z_forward(q, i):
        s = lax.rem(z + LAYERS - i, LAYERS)
        return remote(L.at[q, s], L.at[q, s], zf_s.at[q, i], zf_r.at[q, i], at_layer(up))

    def forward_sends(i):
        return jnp.logical_and(z >= i, z < LAYERS - 1)

    def z_backward(q, i):
        s = lax.rem(z + i, LAYERS)
        return remote(L.at[q, s], L.at[q, s], zb_s.at[q, i], zb_r.at[q, i], at_layer(down))

    def backward_sends(i):
        return lax.rem(z + i, LAYERS) < BACKWARD

    def z_send(q, i):
        if i < FORWARD:
            @pl.when(forward_sends(i))
            def _():
                z_forward(q, i).start()
        if i < BACKWARD:
            @pl.when(backward_sends(i))
            def _():
                z_backward(q, i).start()

    def z_arrive(q, i):
        if i < FORWARD:
            @pl.when(z >= i + 1)
            def _():
                slot = L.at[q, lax.rem(z + LAYERS - 1 - i, LAYERS)]
                remote(slot, slot, zf_s.at[q, i], zf_r.at[q, i], partner).wait_recv()
        if i < BACKWARD:
            @pl.when(lax.rem(z + 1 + i, LAYERS) < BACKWARD)
            def _():
                slot = L.at[q, lax.rem(z + 1 + i, LAYERS)]
                remote(slot, slot, zb_s.at[q, i], zb_r.at[q, i], partner).wait_recv()

    def add(q, s, first):
        if q == 0:
            dec_arrive(s)
            dec_local(s).wait()

        def tile(n, carry):
            cols = pl.ds(pl.multiple_of(n * TILE, TILE), TILE)
            part = jnp.dot(L[q, s], WD[s, :, cols], preferred_element_type=jnp.float32)
            part = part.reshape(SIDE, SIDE, ROWS, TILE)
            if first:
                ACC[q, :, :, :, cols] = part
            else:
                ACC[q, :, :, :, cols] += part
            return carry

        lax.fori_loop(0, D // TILE, tile, 0)

    def z_add(q, i):
        if i < FORWARD:
            @pl.when(z >= i + 1)
            def _():
                add(q, lax.rem(z + LAYERS - 1 - i, LAYERS), False)
        if i < BACKWARD:
            source = lax.rem(z + 1 + i, LAYERS)

            @pl.when(jnp.logical_and(source < BACKWARD, source < z))
            def _():
                add(q, source, False)

    def z_step(q, i):
        z_arrive(q, i)
        z_send(q, i + 1)
        z_add(q, i)

    def line_of(h, offset):
        return move(x, offset) if h == 0 else move(y, offset)

    def place(q, h, k, cols):
        return (q, k, slice(None), slice(None), cols) if h == 0 else (q, slice(None), k, slice(None), cols)

    def neighbour(h, offset):
        return at_chip(move(x, offset), y) if h == 0 else at_chip(x, move(y, offset))

    def rs1(q, h, direction, piece):
        step = 1 if direction == 0 else SIDE - 1
        quarter = direction if piece != 1 else 1 - direction
        cols = pl.ds(h * HALF + quarter * QUARTER, QUARTER)
        src = S.at[place(q, h, line_of(h, 2 if piece == 0 else step), cols)]
        dst = (FA, FB)[h].at[q, direction] if piece == 0 else (TA, TB)[h].at[q, direction, :, :, pl.ds(quarter * QUARTER, QUARTER)]
        return remote(src, dst, rs1_s.at[q, h, direction, piece], rs1_r.at[q, h, direction, piece], neighbour(h, step))

    def rs1_arrive(q, h, direction, piece):
        quarter = direction if piece != 1 else 1 - direction
        slot = (FA, FB)[h].at[q, direction] if piece == 0 else (TA, TB)[h].at[q, direction, :, :, pl.ds(quarter * QUARTER, QUARTER)]
        remote(slot, slot, rs1_s.at[q, h, direction, piece], rs1_r.at[q, h, direction, piece], partner).wait_recv()

    def rs1_start(q):
        def tile(n, carry):
            cols = pl.ds(pl.multiple_of(n * TILE, TILE), TILE)
            S[q, :, :, :, cols] = ACC[q, :, :, :, cols].astype(jnp.bfloat16)
            return carry

        lax.fori_loop(0, D // TILE, tile, 0)
        for piece in range(2):
            for h in range(2):
                for direction in range(2):
                    rs1(q, h, direction, piece).start()

    def rs1_relay(q):
        for h in range(2):
            for direction in range(2):
                step = 1 if direction == 0 else SIDE - 1
                rs1_arrive(q, h, direction, 0)
                at = place(q, h, line_of(h, step), pl.ds(h * HALF + direction * QUARTER, QUARTER))
                far = (FA, FB)[h][q, direction].astype(jnp.float32)
                S[at] = (ACC[at] + far).astype(jnp.bfloat16)
                rs1(q, h, direction, 2).start()

    def rs2(q, h, j):
        o = OFFSETS[j]
        if h == 0:
            return remote(VA.at[q, move(y, o)], UA.at[q, j], rs2_s.at[q, h, j], rs2_r.at[q, h, j], at_chip(x, move(y, o)))
        return remote(VB.at[q, move(x, o)], UB.at[q, j], rs2_s.at[q, h, j], rs2_r.at[q, h, j], at_chip(move(x, o), y))

    def rs2_start(q):
        for h, T, V in ((0, TA, VA), (1, TB, VB)):
            cols = pl.ds(h * HALF, HALF)
            for piece in (1, 2):
                for direction in range(2):
                    rs1_arrive(q, h, direction, piece)

            def line(k, carry):
                at = (q, x, k, slice(None), cols) if h == 0 else (q, k, y, slice(None), cols)
                total = ACC[at]
                for j in range(2):
                    total = total + T[q, j, k].astype(jnp.float32)
                ACC[at] = total
                V[q, k] = total.astype(jnp.bfloat16)
                return carry

            lax.fori_loop(0, SIDE, line, 0)
            for j in (2, 0, 1):
                rs2(q, h, j).start()

    def result(q):
        return pltpu.make_async_copy(OV.at[q], out.at[0, pl.ds(q * ROWS, ROWS), :], out_sem.at[q])

    def finish(q):
        mlp_copy(q).wait()
        for h, U in ((0, UA), (1, UB)):
            cols = pl.ds(h * HALF, HALF)
            for j in (0, 1, 2):
                slot = U.at[q, j]
                remote(slot, slot, rs2_s.at[q, h, j], rs2_r.at[q, h, j], partner).wait_recv()
            total = ACC[q, x, y, :, cols]
            for j in range(3):
                total = total + U[q, j].astype(jnp.float32)
            OV[q, :, cols] = (MV[q, :, cols].astype(jnp.float32) - total).astype(jnp.bfloat16)
        result(q).start()

    def weights(k, carry):
        dec_remote(z - k).start()
        dec_local(z - k).start()
        return carry

    def start(q):
        for copy in enc_pair():
            copy.start()
        for copy in enc_local():
            copy.start()
        for c in range(CHUNKS):
            own_rows(c).start()
        lax.fori_loop(0, z + 1, weights, 0)
        for c in range(CHUNKS):
            mlp_copy(c).start()

    def second(q):
        own_rows(q).wait()
        for h in range(2):
            ag1_wait(q, h)
        for h in range(2):
            ag2_start(q, h)

    def code(q):
        ag2_rest(q)
        encode(q)

    def send(q):
        z_send(q, 0)

    def own(q):
        add(q, z, True)

    steps = {
        "first": ag1_start, "start": start, "second": second, "relay": ag2_relay,
        "code": code, "send": send, "own": own, "rs1": rs1_start, "add": rs1_relay, "rs2": rs2_start, "end": finish,
    }
    for name, q in SCHEDULE:
        if name[0] == "z":
            z_step(q, int(name[1]))
        else:
            steps[name](q)

    for q in range(CHUNKS):
        for h in range(2):
            for j in range(3):
                ag1(q, h, j).wait_send()
                rs2(q, h, j).wait_send()
            for direction in range(2):
                for piece in range(3):
                    ag2(q, h, direction, piece).wait_send()
                    rs1(q, h, direction, piece).wait_send()
        for i in range(FORWARD):
            @pl.when(forward_sends(i))
            def _():
                z_forward(q, i).wait_send()
        for i in range(BACKWARD):
            @pl.when(backward_sends(i))
            def _():
                z_backward(q, i).wait_send()
        result(q).wait()
    for copy in enc_pair():
        copy.wait_send()

    def drained(s, carry):
        dec_remote(s).wait_send()
        return carry

    lax.fori_loop(0, z + 1, drained, 0)


def body(*args):
    bf16, f32 = jnp.bfloat16, jnp.float32
    dma = pltpu.SemaphoreType.DMA
    any_space = pl.BlockSpec(memory_space=pl.ANY)
    block = (CHUNKS, SIDE, SIDE, ROWS, D)
    return pl.pallas_call(
        kernel,
        out_shape=jax.ShapeDtypeStruct(args[0].shape, bf16),
        in_specs=[any_space] * 5,
        out_specs=any_space,
        scratch_shapes=[
            pltpu.VMEM(block, bf16),
            pltpu.VMEM((D, 2 * LANES), bf16),
            pltpu.VMEM((1, 2 * LANES), f32),
            pltpu.VMEM((LAYERS, 2 * LANES, D), bf16),
            pltpu.VMEM((CHUNKS, LAYERS, SIDE * SIDE * ROWS, 2 * LANES), bf16),
            pltpu.VMEM(block, f32),
            pltpu.VMEM(block, bf16),
            pltpu.VMEM((CHUNKS, 2, SIDE, ROWS, QUARTER), bf16),
            pltpu.VMEM((CHUNKS, 2, SIDE, ROWS, QUARTER), bf16),
            pltpu.VMEM((CHUNKS, 2, SIDE, ROWS, HALF), bf16),
            pltpu.VMEM((CHUNKS, 2, SIDE, ROWS, HALF), bf16),
            pltpu.VMEM((CHUNKS, SIDE, ROWS, HALF), bf16),
            pltpu.VMEM((CHUNKS, SIDE, ROWS, HALF), bf16),
            pltpu.VMEM((CHUNKS, 3, ROWS, HALF), bf16),
            pltpu.VMEM((CHUNKS, 3, ROWS, HALF), bf16),
            pltpu.VMEM((CHUNKS, ROWS, D), bf16),
            pltpu.VMEM((CHUNKS, ROWS, D), bf16),
            dma((CHUNKS, 2, 3)), dma((CHUNKS, 2, 3)),
            dma((CHUNKS, 2, 2, 3)), dma((CHUNKS, 2, 2, 3)),
            dma((2,)), dma((2,)),
            dma((LAYERS,)), dma((LAYERS,)),
            dma((CHUNKS, FORWARD)), dma((CHUNKS, FORWARD)),
            dma((CHUNKS, BACKWARD)), dma((CHUNKS, BACKWARD)),
            dma((CHUNKS, 2, 2, 3)), dma((CHUNKS, 2, 2, 3)),
            dma((CHUNKS, 2, 3)), dma((CHUNKS, 2, 3)),
            dma((CHUNKS,)), dma((CHUNKS,)), dma((2,)), dma((LAYERS,)), dma((CHUNKS,)),
        ],
        compiler_params=pltpu.CompilerParams(
            collective_id=0, has_side_effects=True, vmem_limit_bytes=60 * 2**20
        ),
    )(*args)


def solution(mesh):
    return jax.shard_map(
        body,
        mesh=mesh,
        in_specs=(
            P("layer", "latent", None),
            P("layer", "latent", None),
            P("layer", None, "latent"),
            P("layer", "latent"),
            P("layer", None, "latent", None),
        ),
        out_specs=P("layer", "latent", None),
        check_vma=False,
    )
```
